32 devices in a mesh: dp: 4 (over x, core), cls: 8 (over z, y).
Axes of the slice: x: 2, y: 2, z: 4, core: 2. Of those that a mesh axis runs over, the one named last changes fastest.
Arguments:
- faces: bfloat16 [2, 32, 512], P(None, ('dp', 'cls')), may hold values from -2 to 2
- labels: int32 [2, 32], replicated, may hold values from 0 to 16383, as said below
- centres: bfloat16 [16384, 512], P(('dp', 'cls')), may hold values from -4 to 4
- momentum: bfloat16 [16384, 512], P(('dp', 'cls')), may hold values from -3 to 3
Outputs:
- face_grad: float32 [2, 32, 512], P(None, ('dp', 'cls'))
- new_centres: bfloat16 [16384, 512], P(('dp', 'cls'))
- new_momentum: bfloat16 [16384, 512], P(('dp', 'cls'))
The draws below stay inside these ranges and needn't reach their ends.
Inputs may be any that keep to these rules, and one draw needn't show every extreme that they name: `labels`: some face has class 0 and some face has class 16384 - 1.
All inputs are finite; a program needn't handle non-finite values.
Results may differ from the reference program's by a relative error of at most 0.0057.
Values may be sent and summed in bfloat16 or wider, within the bound.
A program may use at most 64 MiB of HBM per device.

```python
import math
import jax
import jax.numpy as jnp
from jax import lax

D = 512
CLS_DEV = 512
MB = 2
FACES = 32
CLASSES = 16384


cluster_count = 256


def unit_noise(key, shape):
    values = jnp.clip(jax.random.normal(key, shape, jnp.float32), -4.0, 4.0)
    return values


def class_directions(key, class_ids):
    inverse_root = 1.0 / math.sqrt(D)
    cluster_means = unit_noise(jax.random.fold_in(key, 102), (cluster_count, D)) * inverse_root
    top_share = 0.6
    class_base = jax.random.fold_in(key, 101)

    def one_class(class_id):
        row_key = jax.random.fold_in(class_base, class_id)
        cluster = jax.random.randint(jax.random.fold_in(row_key, 1), (), 0, cluster_count)
        share = jax.random.uniform(jax.random.fold_in(row_key, 2), (), jnp.float32, 0.0, top_share)
        noise = unit_noise(jax.random.fold_in(row_key, 3), (D,)) * inverse_root
        return share * cluster_means[cluster] + jnp.sqrt(1.0 - share * share) * noise
    return jax.vmap(one_class)(class_ids)


def face_labels(key):
    drawn = jax.random.randint(jax.random.fold_in(key, 201), (MB * FACES,), 0, CLASSES)
    spots = jax.random.permutation(jax.random.fold_in(key, 202), MB * FACES)
    drawn = drawn.at[spots[0]].set(0)
    drawn = drawn.at[spots[1]].set(CLASSES - 1)
    return drawn.reshape(MB, FACES).astype(jnp.int32)


def draw_labels(key, part):
    return face_labels(key)


def draw_centres(key, part):
    directions = class_directions(key, jnp.arange(CLASSES, dtype=jnp.int32))
    scale_key = jax.random.fold_in(key, 103)
    row_scale = jax.random.uniform(scale_key, (CLASSES, 1), jnp.float32, 0.8, 1.25)
    return (row_scale * directions).astype(jnp.bfloat16)


def draw_faces(key, part):
    flat_labels = face_labels(key).reshape(-1)
    directions = class_directions(key, flat_labels)
    near_lo = 0.5
    near_hi = 0.9
    nearness = jax.random.uniform(jax.random.fold_in(key, 301), (MB * FACES, 1), jnp.float32, near_lo, near_hi)
    noise = unit_noise(jax.random.fold_in(key, 302), (MB * FACES, D)) * (1.0 / math.sqrt(D))
    result = nearness * directions + jnp.sqrt(1.0 - nearness * nearness) * noise
    return result.reshape(MB, FACES, D).astype(jnp.bfloat16)


def shard_levels(key, extent, shards, smallest, high):
    level = 1.0
    for axis_at, blocks in shards:
        heights = jax.random.uniform(jax.random.fold_in(jax.random.fold_in(key, 6), axis_at), (blocks,), jnp.float32, smallest / len(shards), high / len(shards))
        level = level * jnp.repeat(jnp.exp(heights), extent[axis_at] // blocks).reshape((-1,) + (1,) * (len(extent) - 1 - axis_at))
    return level


def scatter_about(rng, dims, scale, reach, cuts=(), kind=jnp.bfloat16):
    factor_of = shard_levels(rng, dims, cuts, -0.22, 0.18) if cuts else 1.0
    values = jax.random.normal(rng, dims, jnp.float32) * scale * factor_of
    return jnp.minimum(jnp.maximum(values, -reach), reach).astype(kind)


def setup_inputs(seed: int = 0) -> dict:
    key_list = jax.random.split(jax.random.key(seed), 5)
    return {
        "faces": draw_faces(jax.random.fold_in(key_list[4], 71), 0),
        "labels": draw_labels(jax.random.fold_in(key_list[4], 71), 0),
        "centres": draw_centres(jax.random.fold_in(key_list[4], 71), 0),
        "momentum": scatter_about(key_list[3], (CLASSES, D), 0.5, 3.0, ((0, 32),)),
    }


SCALE = 30.0
MARGIN = 0.4
POS_WEIGHT = 0.7
BIAS = 6.5
EPS = 1e-06
MOMENTUM_RATE = 0.9
LEARN_RATE = 0.1
DECAY = 0.0005

def logit_grad(cosine, positive):
    halfway = (cosine + 1.0) * 0.5
    shaped = 2.0 * halfway * halfway * halfway - 1.0
    slopes = 3.0 * halfway * halfway
    pos_term = -POS_WEIGHT * SCALE * jax.nn.sigmoid(-(SCALE * (shaped - MARGIN) + BIAS))
    neg_term = (1.0 - POS_WEIGHT) * SCALE * jax.nn.sigmoid(SCALE * (shaped + MARGIN) + BIAS)
    return (jnp.where(positive, pos_term, neg_term) * slopes).astype(jnp.bfloat16)

def normalize(centres):
    master = centres.astype(jnp.float32)
    length = jnp.sqrt(lax.optimization_barrier(jnp.sum(master * master, axis=1, keepdims=True)) + EPS)
    return (master, length, master / length)

def update(master, length, unit_wide, grad_unit, momentum):
    radial = lax.optimization_barrier(jnp.sum(unit_wide * grad_unit, axis=1, keepdims=True))
    grad_centre = (grad_unit - unit_wide * radial) / length
    velocity = MOMENTUM_RATE * momentum.astype(jnp.float32) + grad_centre + DECAY * master
    return ((master - LEARN_RATE * velocity).astype(jnp.bfloat16), velocity.astype(jnp.bfloat16))

def reference(faces, labels, centres, momentum):
    width = centres.shape[1]
    blocks = centres.shape[0] // CLS_DEV
    centre_blocks = centres.reshape(blocks, CLS_DEV, width)
    moment_blocks = momentum.reshape(blocks, CLS_DEV, width)
    bases = jnp.arange(blocks, dtype=jnp.int32) * CLS_DEV

    def step(totals, inputs):
        block_centres, block_moment, base = inputs
        master, length, unit_wide = normalize(block_centres)
        unit_rows = unit_wide.astype(jnp.bfloat16)
        class_ids = base + jnp.arange(CLS_DEV, dtype=jnp.int32)
        grad_unit = jnp.zeros((CLS_DEV, width), jnp.float32)
        new_totals = []
        for batch_number in range(MB):
            cosine = jnp.dot(faces[batch_number], unit_rows.T, preferred_element_type=jnp.float32)
            positive = labels[batch_number][:, None] == class_ids[None, :]
            dlogit = logit_grad(cosine, positive)
            grad_unit = grad_unit + jnp.dot(dlogit.T, faces[batch_number], preferred_element_type=jnp.float32)
            new_totals.append(totals[batch_number] + jnp.dot(dlogit, unit_rows, preferred_element_type=jnp.float32))
        new_c, new_m = update(master, length, unit_wide, grad_unit, block_moment)
        return (jnp.stack(new_totals), (new_c, new_m))
    start_totals = jnp.zeros((MB, faces.shape[1], width), jnp.float32)
    face_grad, outs = lax.scan(step, start_totals, (centre_blocks, moment_blocks, bases))
    return (face_grad, outs[0].reshape(-1, width), outs[1].reshape(-1, width))
```

```python
import functools
import jax
import jax.numpy as jnp
from jax import lax
from jax.experimental import pallas as pl
from jax.experimental.pallas import tpu as pltpu
from jax.sharding import PartitionSpec as P

SCALE = 30.0
MARGIN = 0.4
POS_WEIGHT = 0.7
BIAS = 6.5
EPS = 1e-06
MOMENTUM_RATE = 0.9
LEARN_RATE = 0.1
DECAY = 0.0005
MESH = pl.DeviceIdType.MESH


def logit_grad(cosine, positive):
    halfway = (cosine + 1.0) * 0.5
    square = halfway * halfway
    shaped = 2.0 * square * halfway - 1.0
    slopes = 3.0 * square
    argument = jnp.where(
        positive, -(SCALE * (shaped - MARGIN) + BIAS), SCALE * (shaped + MARGIN) + BIAS
    )
    weight = jnp.where(positive, -POS_WEIGHT * SCALE, (1.0 - POS_WEIGHT) * SCALE)
    return (weight * jax.nn.sigmoid(argument) * slopes).astype(jnp.bfloat16)


def kernel(
    devices, group, face_rows, chunk, block,
    faces_hbm, labels_hbm, centres_hbm, momentum_hbm,
    face_grad, new_centres_hbm, new_momentum_hbm,
    raw, own, gathered, labels, centres, momentum, unit, inverse, grad, outgoing, incoming,
    new_centres, new_momentum,
    local_sems, gather_send, gather_recv, scatter_send, scatter_recv,
):
    outer, inner = lax.axis_index("dp"), lax.axis_index("cls")
    me = outer * group + inner
    rows, width = centres.shape
    batches = raw.shape[0]
    slot_rows = batches * face_rows

    def device(index):
        return (index // group, index % group)

    load_faces = pltpu.make_async_copy(faces_hbm, raw, local_sems.at[0])
    load_labels = pltpu.make_async_copy(labels_hbm, labels, local_sems.at[1])
    load_centres = pltpu.make_async_copy(centres_hbm, centres, local_sems.at[2])
    load_momentum = pltpu.make_async_copy(momentum_hbm, momentum, local_sems.at[3])
    load_faces.start()
    load_centres.start()
    load_labels.start()
    load_momentum.start()

    barrier = pltpu.get_barrier_semaphore()

    def greet(step, carry):
        peer = lax.rem(me + step, devices)
        pl.semaphore_signal(barrier, inc=1, device_id=device(peer), device_id_type=MESH)
        return carry

    lax.fori_loop(1, devices, greet, 0)
    load_faces.wait()
    own[...] = raw[...].reshape(slot_rows, width)
    pl.semaphore_wait(barrier, devices - 1)

    def gather(step, carry):
        peer = lax.rem(me + step, devices)
        pltpu.make_async_remote_copy(
            src_ref=own, dst_ref=gathered.at[me], send_sem=gather_send, recv_sem=gather_recv,
            device_id=device(peer), device_id_type=MESH,
        ).start()
        return carry

    lax.fori_loop(1, devices, gather, 0)
    pltpu.make_async_copy(own, gathered.at[me], gather_recv).start()

    load_centres.wait()

    def normalize(step, carry):
        part = pl.ds(pl.multiple_of(step * block, block), block)
        master = centres[part, :].astype(jnp.float32)
        scale = lax.rsqrt(jnp.sum(master * master, axis=1, keepdims=True) + EPS)
        inverse[part, :] = scale
        unit[part, :] = (master * scale).astype(jnp.bfloat16)
        return carry

    lax.fori_loop(0, rows // block, normalize, 0)
    load_labels.wait()
    count = chunk * slot_rows
    class_ids = me * rows + lax.broadcasted_iota(jnp.int32, (count, rows), 1)

    def label_column(first):
        shape = (count, labels.shape[1])
        row = lax.broadcasted_iota(jnp.int32, shape, 0)
        lane = lax.broadcasted_iota(jnp.int32, shape, 1)
        inside = row % slot_rows
        wanted = (first + row // slot_rows) * face_rows + inside % face_rows
        batch = inside // face_rows
        values = jnp.zeros(shape, jnp.float32)
        for number in range(batches):
            line = labels[number : number + 1, :].astype(jnp.float32)
            values = jnp.where((lane == wanted) & (batch == number), line, values)
        return jnp.sum(values, axis=1, keepdims=True).astype(jnp.int32)

    chunks = devices // chunk
    if chunks == 1:
        column = label_column(0)
    pltpu.make_async_copy(gathered, gathered, gather_recv).wait()

    def fold(step):
        if chunks == 1:
            slots = slice(None)
            target = column
        else:
            slots = pl.ds(step * chunk, chunk)
            target = label_column(step * chunk)
        piece = gathered[slots].reshape(count, width)
        cosine = lax.dot_general(
            piece, unit[...], (((1,), (1,)), ((), ())), preferred_element_type=jnp.float32
        )
        dlogit = logit_grad(cosine, target == class_ids)
        term = jnp.dot(dlogit, unit[...], preferred_element_type=jnp.float32)
        outgoing[slots] = term.astype(jnp.bfloat16).reshape(chunk, slot_rows, width)
        return dlogit, piece

    def outer_product(dlogit, piece):
        return lax.dot_general(
            dlogit, piece, (((0,), (0,)), ((), ())), preferred_element_type=jnp.float32
        )

    def scatter(step, carry):
        peer = lax.rem(me + step, devices)
        pltpu.make_async_remote_copy(
            src_ref=outgoing.at[peer], dst_ref=incoming.at[me],
            send_sem=scatter_send, recv_sem=scatter_recv,
            device_id=device(peer), device_id_type=MESH,
        ).start()
        return carry

    if chunks == 1:
        dlogit, piece = fold(0)
        lax.fori_loop(1, devices, scatter, 0)
        pltpu.make_async_copy(outgoing.at[me], incoming.at[me], scatter_recv).start()
        grad[...] = outer_product(dlogit, piece)
    else:
        grad[...] = jnp.zeros_like(grad)

        def step_chunk(step, carry):
            dlogit, piece = fold(step)
            grad[...] += outer_product(dlogit, piece)
            return carry

        lax.fori_loop(0, chunks, step_chunk, 0)
        lax.fori_loop(1, devices, scatter, 0)
        pltpu.make_async_copy(outgoing.at[me], incoming.at[me], scatter_recv).start()

    load_momentum.wait()

    def update(step, carry):
        part = pl.ds(pl.multiple_of(step * block, block), block)
        master = centres[part, :].astype(jnp.float32)
        scale = inverse[part, :]
        wide = master * scale
        grad_unit = grad[part, :]
        radial = jnp.sum(wide * grad_unit, axis=1, keepdims=True)
        grad_centre = (grad_unit - wide * radial) * scale
        velocity = (
            MOMENTUM_RATE * momentum[part, :].astype(jnp.float32) + grad_centre + DECAY * master
        )
        new_centres[part, :] = (master - LEARN_RATE * velocity).astype(jnp.bfloat16)
        new_momentum[part, :] = velocity.astype(jnp.bfloat16)
        return carry

    lax.fori_loop(0, rows // block, update, 0)
    store_centres = pltpu.make_async_copy(new_centres, new_centres_hbm, local_sems.at[4])
    store_momentum = pltpu.make_async_copy(new_momentum, new_momentum_hbm, local_sems.at[5])
    store_centres.start()
    store_momentum.start()

    pltpu.make_async_copy(incoming, incoming, scatter_recv).wait()
    if chunks == 1:
        total = jnp.sum(incoming[...].astype(jnp.float32), axis=0)
    else:
        total = lax.fori_loop(
            0, chunks,
            lambda step, sofar: sofar
            + jnp.sum(incoming[pl.ds(step * chunk, chunk)].astype(jnp.float32), axis=0),
            jnp.zeros((slot_rows, width), jnp.float32),
        )
    face_grad[...] = total.reshape(batches, face_rows, width)

    if devices > 1:
        others = gathered.at[pl.ds(0, devices - 1)]
        pltpu.make_async_copy(others, others, gather_send).wait()
        others = outgoing.at[pl.ds(0, devices - 1)]
        pltpu.make_async_copy(others, others, scatter_send).wait()
    store_centres.wait()
    store_momentum.wait()


def local(devices, group, faces, labels, centres, momentum):
    batches, face_rows, width = faces.shape
    rows = centres.shape[0]
    slot_rows = batches * face_rows
    chunk = devices
    while chunk * slot_rows > 64 and chunk % 2 == 0:
        chunk //= 2
    block = 64 if rows % 64 == 0 else rows
    half = jnp.bfloat16
    hbm = pl.BlockSpec(memory_space=pltpu.HBM)
    slots = pltpu.VMEM((devices, slot_rows, width), half)
    square = pltpu.VMEM((rows, width), half)
    return pl.pallas_call(
        functools.partial(kernel, devices, group, face_rows, chunk, block),
        out_shape=(
            jax.ShapeDtypeStruct(faces.shape, jnp.float32),
            jax.ShapeDtypeStruct(centres.shape, half),
            jax.ShapeDtypeStruct(momentum.shape, half),
        ),
        in_specs=[hbm] * 4,
        out_specs=(pl.BlockSpec(memory_space=pltpu.VMEM), hbm, hbm),
        scratch_shapes=[
            pltpu.VMEM(faces.shape, half),
            pltpu.VMEM((slot_rows, width), half),
            slots,
            pltpu.VMEM(labels.shape, jnp.int32),
            square, square, square,
            pltpu.VMEM((rows, 1), jnp.float32),
            pltpu.VMEM((rows, width), jnp.float32),
            slots, slots,
            square, square,
            pltpu.SemaphoreType.DMA((6,)),
            pltpu.SemaphoreType.DMA,
            pltpu.SemaphoreType.DMA,
            pltpu.SemaphoreType.DMA,
            pltpu.SemaphoreType.DMA,
        ],
        compiler_params=pltpu.CompilerParams(collective_id=0, has_side_effects=True),
    )(faces, labels, centres, momentum)


def solution(mesh):
    group = mesh.shape["cls"]
    devices = mesh.shape["dp"] * group
    in_specs = (P(None, ("dp", "cls"), None), P(), P(("dp", "cls"), None), P(("dp", "cls"), None))
    out_specs = (P(None, ("dp", "cls"), None), P(("dp", "cls"), None), P(("dp", "cls"), None))
    return jax.shard_map(
        functools.partial(local, devices, group),
        mesh=mesh, in_specs=in_specs, out_specs=out_specs, check_vma=False,
    )
```

```python
import functools
import jax
import jax.numpy as jnp
from jax import lax
from jax.experimental import pallas as pl
from jax.experimental.pallas import tpu as pltpu
from jax.sharding import PartitionSpec as P

SCALE = 30.0
MARGIN = 0.4
POS_WEIGHT = 0.7
BIAS = 6.5
EPS = 1e-06
MOMENTUM_RATE = 0.9
LEARN_RATE = 0.1
DECAY = 0.0005
MESH = pl.DeviceIdType.MESH


def logit_grad(cosine, positive):
    halfway = (cosine + 1.0) * 0.5
    square = halfway * halfway
    shaped = 2.0 * square * halfway - 1.0
    slopes = 3.0 * square
    argument = jnp.where(
        positive, -(SCALE * (shaped - MARGIN) + BIAS), SCALE * (shaped + MARGIN) + BIAS
    )
    weight = jnp.where(positive, -POS_WEIGHT * SCALE, (1.0 - POS_WEIGHT) * SCALE)
    return (weight * jax.nn.sigmoid(argument) * slopes).astype(jnp.bfloat16)


def kernel(
    devices, group, face_rows, chunk, block,
    faces_hbm, labels_hbm, centres_hbm, momentum_hbm,
    face_grad, new_centres, new_momentum,
    own, gathered, labels, centres, momentum, unit, inverse, grad, outgoing, incoming,
    local_sems, gather_send, gather_recv, scatter_send, scatter_recv,
):
    outer, inner = lax.axis_index("dp"), lax.axis_index("cls")
    me = outer * group + inner
    rows, width = centres.shape
    batches = labels.shape[0]
    slot_rows = batches * face_rows

    def device(index):
        return (index // group, index % group)

    load_faces = pltpu.make_async_copy(faces_hbm, own, local_sems.at[0])
    load_labels = pltpu.make_async_copy(labels_hbm, labels, local_sems.at[1])
    load_centres = pltpu.make_async_copy(centres_hbm, centres, local_sems.at[2])
    load_momentum = pltpu.make_async_copy(momentum_hbm, momentum, local_sems.at[3])
    load_faces.start()
    load_centres.start()
    load_labels.start()
    load_momentum.start()

    barrier = pltpu.get_barrier_semaphore()

    def greet(step, carry):
        peer = lax.rem(me + step, devices)
        pl.semaphore_signal(barrier, inc=1, device_id=device(peer), device_id_type=MESH)
        return carry

    lax.fori_loop(1, devices, greet, 0)
    load_faces.wait()
    pl.semaphore_wait(barrier, devices - 1)

    def gather(step, carry):
        peer = lax.rem(me + step, devices)
        pltpu.make_async_remote_copy(
            src_ref=own, dst_ref=gathered.at[me], send_sem=gather_send, recv_sem=gather_recv,
            device_id=device(peer), device_id_type=MESH,
        ).start()
        return carry

    lax.fori_loop(1, devices, gather, 0)
    pltpu.make_async_copy(own, gathered.at[me], gather_recv).start()

    load_centres.wait()

    def normalize(step, carry):
        part = pl.ds(pl.multiple_of(step * block, block), block)
        master = centres[part, :].astype(jnp.float32)
        scale = lax.rsqrt(jnp.sum(master * master, axis=1, keepdims=True) + EPS)
        inverse[part, :] = scale
        unit[part, :] = (master * scale).astype(jnp.bfloat16)
        return carry

    lax.fori_loop(0, rows // block, normalize, 0)
    load_labels.wait()
    count = chunk * slot_rows
    class_ids = me * rows + lax.broadcasted_iota(jnp.int32, (count, rows), 1)

    def label_column(first):
        shape = (count, labels.shape[1])
        row = lax.broadcasted_iota(jnp.int32, shape, 0)
        lane = lax.broadcasted_iota(jnp.int32, shape, 1)
        wanted = first * face_rows + row // batches
        batch = row % batches
        values = jnp.zeros(shape, jnp.float32)
        for number in range(batches):
            line = labels[number : number + 1, :].astype(jnp.float32)
            values = jnp.where((lane == wanted) & (batch == number), line, values)
        return jnp.sum(values, axis=1, keepdims=True).astype(jnp.int32)

    chunks = devices // chunk
    if chunks == 1:
        column = label_column(0)
    pltpu.make_async_copy(gathered, gathered, gather_recv).wait()

    def fold(step):
        if chunks == 1:
            slots = slice(None)
            target = column
        else:
            slots = pl.ds(step * chunk, chunk)
            target = label_column(step * chunk)
        piece = gathered[slots].reshape(count, width)
        cosine = lax.dot_general(
            piece, unit[...], (((1,), (1,)), ((), ())), preferred_element_type=jnp.float32
        )
        dlogit = logit_grad(cosine, target == class_ids)
        term = jnp.dot(dlogit, unit[...], preferred_element_type=jnp.float32)
        outgoing[slots] = term.astype(jnp.bfloat16).reshape(chunk, slot_rows, width)
        return dlogit, piece

    def outer_product(dlogit, piece):
        return lax.dot_general(
            dlogit, piece, (((0,), (0,)), ((), ())), preferred_element_type=jnp.float32
        )

    def scatter(step, carry):
        peer = lax.rem(me + step, devices)
        pltpu.make_async_remote_copy(
            src_ref=outgoing.at[peer], dst_ref=incoming.at[me],
            send_sem=scatter_send, recv_sem=scatter_recv,
            device_id=device(peer), device_id_type=MESH,
        ).start()
        return carry

    if chunks == 1:
        dlogit, piece = fold(0)
        lax.fori_loop(1, devices, scatter, 0)
        pltpu.make_async_copy(outgoing.at[me], incoming.at[me], scatter_recv).start()
        grad[...] = outer_product(dlogit, piece)
    else:
        grad[...] = jnp.zeros_like(grad)

        def step_chunk(step, carry):
            dlogit, piece = fold(step)
            grad[...] += outer_product(dlogit, piece)
            return carry

        lax.fori_loop(0, chunks, step_chunk, 0)
        lax.fori_loop(1, devices, scatter, 0)
        pltpu.make_async_copy(outgoing.at[me], incoming.at[me], scatter_recv).start()

    load_momentum.wait()

    def update(step, carry):
        part = pl.ds(pl.multiple_of(step * block, block), block)
        master = centres[part, :].astype(jnp.float32)
        scale = inverse[part, :]
        wide = master * scale
        grad_unit = grad[part, :]
        radial = jnp.sum(wide * grad_unit, axis=1, keepdims=True)
        grad_centre = (grad_unit - wide * radial) * scale
        velocity = (
            MOMENTUM_RATE * momentum[part, :].astype(jnp.float32) + grad_centre + DECAY * master
        )
        new_centres[part, :] = (master - LEARN_RATE * velocity).astype(jnp.bfloat16)
        new_momentum[part, :] = velocity.astype(jnp.bfloat16)
        return carry

    lax.fori_loop(0, rows // block, update, 0)
    pltpu.make_async_copy(incoming, incoming, scatter_recv).wait()
    if chunks == 1:
        total = jnp.sum(incoming[...].astype(jnp.float32), axis=0)
    else:
        total = lax.fori_loop(
            0, chunks,
            lambda step, sofar: sofar
            + jnp.sum(incoming[pl.ds(step * chunk, chunk)].astype(jnp.float32), axis=0),
            jnp.zeros((slot_rows, width), jnp.float32),
        )
    total = total.reshape(face_rows, batches, width)
    for batch in range(batches):
        face_grad[batch] = total[:, batch, :]

    if devices > 1:
        others = gathered.at[pl.ds(0, devices - 1)]
        pltpu.make_async_copy(others, others, gather_send).wait()
        others = outgoing.at[pl.ds(0, devices - 1)]
        pltpu.make_async_copy(others, others, scatter_send).wait()


def local(devices, group, faces, labels, centres, momentum):
    batches, face_rows, width = faces.shape
    rows = centres.shape[0]
    slot_rows = batches * face_rows
    chunk = devices
    while chunk * slot_rows > 64 and chunk % 2 == 0:
        chunk //= 2
    block = 64 if rows % 64 == 0 else rows
    half = jnp.bfloat16
    hbm = pl.BlockSpec(memory_space=pltpu.HBM)
    vmem = pl.BlockSpec(memory_space=pltpu.VMEM)
    slots = pltpu.VMEM((devices, slot_rows, width), half)
    square = pltpu.VMEM((rows, width), half)
    return pl.pallas_call(
        functools.partial(kernel, devices, group, face_rows, chunk, block),
        out_shape=(
            pltpu.VMEM(faces.shape, jnp.float32),
            pltpu.VMEM(centres.shape, half),
            pltpu.VMEM(momentum.shape, half),
        ),
        in_specs=[hbm] * 4,
        out_specs=(vmem, vmem, vmem),
        scratch_shapes=[
            pltpu.VMEM((slot_rows, width), half),
            slots,
            pltpu.VMEM(labels.shape, jnp.int32),
            square, square, square,
            pltpu.VMEM((rows, 1), jnp.float32),
            pltpu.VMEM((rows, width), jnp.float32),
            slots, slots,
            pltpu.SemaphoreType.DMA((4,)),
            pltpu.SemaphoreType.DMA,
            pltpu.SemaphoreType.DMA,
            pltpu.SemaphoreType.DMA,
            pltpu.SemaphoreType.DMA,
        ],
        compiler_params=pltpu.CompilerParams(collective_id=0, has_side_effects=True),
    )(faces.transpose(1, 0, 2).reshape(slot_rows, width), labels, centres, momentum)


def solution(mesh):
    group = mesh.shape["cls"]
    devices = mesh.shape["dp"] * group
    in_specs = (P(None, ("dp", "cls"), None), P(), P(("dp", "cls"), None), P(("dp", "cls"), None))
    out_specs = (P(None, ("dp", "cls"), None), P(("dp", "cls"), None), P(("dp", "cls"), None))
    return jax.shard_map(
        functools.partial(local, devices, group),
        mesh=mesh, in_specs=in_specs, out_specs=out_specs, check_vma=False,
    )
```

```python
import functools
import jax
import jax.numpy as jnp
from jax import lax
from jax.experimental import pallas as pl
from jax.experimental.pallas import tpu as pltpu
from jax.sharding import PartitionSpec as P

SCALE = 30.0
MARGIN = 0.4
POS_WEIGHT = 0.7
BIAS = 6.5
EPS = 1e-06
MOMENTUM_RATE = 0.9
LEARN_RATE = 0.1
DECAY = 0.0005
MESH = pl.DeviceIdType.MESH


def logit_grad(cosine, positive):
    halfway = (cosine + 1.0) * 0.5
    square = halfway * halfway
    shaped = 2.0 * square * halfway - 1.0
    slopes = 3.0 * square
    argument = jnp.where(
        positive, -(SCALE * (shaped - MARGIN) + BIAS), SCALE * (shaped + MARGIN) + BIAS
    )
    weight = jnp.where(positive, -POS_WEIGHT * SCALE, (1.0 - POS_WEIGHT) * SCALE)
    return (weight * jax.nn.sigmoid(argument) * slopes).astype(jnp.bfloat16)


def kernel(
    devices, group, face_rows, chunk, block,
    faces_hbm, labels_hbm, centres_hbm, momentum_hbm,
    face_grad, new_centres, new_momentum,
    own, gathered, labels, centres, momentum, unit, inverse, grad, outgoing, incoming,
    local_sems, gather_send, gather_recv, scatter_send, scatter_recv,
):
    outer, inner = lax.axis_index("dp"), lax.axis_index("cls")
    me = outer * group + inner
    rows, width = centres.shape
    batches = labels.shape[0]
    slot_rows = batches * face_rows

    def device(index):
        return (index // group, index % group)

    load_faces = pltpu.make_async_copy(faces_hbm, own, local_sems.at[0])
    load_labels = pltpu.make_async_copy(labels_hbm, labels, local_sems.at[1])
    load_centres = pltpu.make_async_copy(centres_hbm, centres, local_sems.at[2])
    load_momentum = pltpu.make_async_copy(momentum_hbm, momentum, local_sems.at[3])
    load_faces.start()
    load_centres.start()
    load_labels.start()
    load_momentum.start()

    barrier = pltpu.get_barrier_semaphore()

    def greet(step, carry):
        peer = lax.rem(me + step, devices)
        pl.semaphore_signal(barrier, inc=1, device_id=device(peer), device_id_type=MESH)
        return carry

    lax.fori_loop(1, devices, greet, 0)
    load_faces.wait()
    pl.semaphore_wait(barrier, devices - 1)

    def gather(step, carry):
        peer = lax.rem(me + step, devices)
        pltpu.make_async_remote_copy(
            src_ref=own, dst_ref=gathered.at[me], send_sem=gather_send, recv_sem=gather_recv,
            device_id=device(peer), device_id_type=MESH,
        ).start()
        return carry

    lax.fori_loop(1, devices, gather, 0)
    pltpu.make_async_copy(own, gathered.at[me], gather_recv).start()

    load_centres.wait()

    def normalize(step, carry):
        part = pl.ds(pl.multiple_of(step * block, block), block)
        master = centres[part, :].astype(jnp.float32)
        scale = lax.rsqrt(jnp.sum(master * master, axis=1, keepdims=True) + EPS)
        inverse[part, :] = scale
        unit[part, :] = (master * scale).astype(jnp.bfloat16)
        return carry

    lax.fori_loop(0, rows // block, normalize, 0)
    load_labels.wait()
    count = chunk * slot_rows
    class_ids = me * rows + lax.broadcasted_iota(jnp.int32, (count, rows), 1)

    def label_column(first):
        shape = (count, labels.shape[1])
        row = lax.broadcasted_iota(jnp.int32, shape, 0)
        lane = lax.broadcasted_iota(jnp.int32, shape, 1)
        wanted = first * face_rows + row // batches
        batch = row % batches
        values = jnp.zeros(shape, jnp.float32)
        for number in range(batches):
            line = labels[number : number + 1, :].astype(jnp.float32)
            values = jnp.where((lane == wanted) & (batch == number), line, values)
        return jnp.sum(values, axis=1, keepdims=True).astype(jnp.int32)

    chunks = devices // chunk
    if chunks == 1:
        column = label_column(0)
    pltpu.make_async_copy(gathered, gathered, gather_recv).wait()

    def fold(step):
        if chunks == 1:
            slots = slice(None)
            target = column
        else:
            slots = pl.ds(step * chunk, chunk)
            target = label_column(step * chunk)
        piece = gathered[slots].reshape(count, width)
        cosine = lax.dot_general(
            piece, unit[...], (((1,), (1,)), ((), ())), preferred_element_type=jnp.float32
        )
        dlogit = logit_grad(cosine, target == class_ids)
        term = jnp.dot(dlogit, unit[...], preferred_element_type=jnp.float32)
        outgoing[slots] = term.astype(jnp.bfloat16).reshape(chunk, slot_rows, width)
        return dlogit, piece

    def outer_product(dlogit, piece):
        return lax.dot_general(
            dlogit, piece, (((0,), (0,)), ((), ())), preferred_element_type=jnp.float32
        )

    def scatter(step, carry):
        peer = lax.rem(me + step, devices)
        pltpu.make_async_remote_copy(
            src_ref=outgoing.at[peer], dst_ref=incoming.at[me],
            send_sem=scatter_send, recv_sem=scatter_recv,
            device_id=device(peer), device_id_type=MESH,
        ).start()
        return carry

    if chunks == 1:
        dlogit, piece = fold(0)
        lax.fori_loop(1, devices, scatter, 0)
        pltpu.make_async_copy(outgoing.at[me], incoming.at[me], scatter_recv).start()
        grad[...] = outer_product(dlogit, piece)
    else:
        grad[...] = jnp.zeros_like(grad)

        def step_chunk(step, carry):
            dlogit, piece = fold(step)
            grad[...] += outer_product(dlogit, piece)
            return carry

        lax.fori_loop(0, chunks, step_chunk, 0)
        lax.fori_loop(1, devices, scatter, 0)
        pltpu.make_async_copy(outgoing.at[me], incoming.at[me], scatter_recv).start()

    load_momentum.wait()

    def update(step, carry):
        part = pl.ds(pl.multiple_of(step * block, block), block)
        master = centres[part, :].astype(jnp.float32)
        scale = inverse[part, :]
        wide = master * scale
        grad_unit = grad[part, :]
        radial = jnp.sum(wide * grad_unit, axis=1, keepdims=True)
        grad_centre = (grad_unit - wide * radial) * scale
        velocity = (
            MOMENTUM_RATE * momentum[part, :].astype(jnp.float32) + grad_centre + DECAY * master
        )
        new_centres[part, :] = (master - LEARN_RATE * velocity).astype(jnp.bfloat16)
        new_momentum[part, :] = velocity.astype(jnp.bfloat16)
        return carry

    lax.fori_loop(0, rows // block, update, 0)
    pltpu.make_async_copy(incoming, incoming, scatter_recv).wait()
    if chunks == 1:
        total = jnp.sum(incoming[...].astype(jnp.float32), axis=0)
    else:
        total = lax.fori_loop(
            0, chunks,
            lambda step, sofar: sofar
            + jnp.sum(incoming[pl.ds(step * chunk, chunk)].astype(jnp.float32), axis=0),
            jnp.zeros((slot_rows, width), jnp.float32),
        )
    total = total.reshape(face_rows, batches, width)
    for batch in range(batches):
        face_grad[batch] = total[:, batch, :]

    if devices > 1:
        others = gathered.at[pl.ds(0, devices - 1)]
        pltpu.make_async_copy(others, others, gather_send).wait()
        others = outgoing.at[pl.ds(0, devices - 1)]
        pltpu.make_async_copy(others, others, scatter_send).wait()


def store_kernel(*refs):
    count = (len(refs) - 1) // 2
    sems = refs[-1]
    stores = [
        pltpu.make_async_copy(refs[number], refs[count + number], sems.at[number])
        for number in range(count)
    ]
    for store in stores:
        store.start()
    for store in stores:
        store.wait()


def local(devices, group, faces, labels, centres, momentum):
    batches, face_rows, width = faces.shape
    rows = centres.shape[0]
    slot_rows = batches * face_rows
    chunk = devices
    while chunk * slot_rows > 64 and chunk % 2 == 0:
        chunk //= 2
    block = 64 if rows % 64 == 0 else rows
    half = jnp.bfloat16
    hbm = pl.BlockSpec(memory_space=pltpu.HBM)
    vmem = pl.BlockSpec(memory_space=pltpu.VMEM)
    slots = pltpu.VMEM((devices, slot_rows, width), half)
    square = pltpu.VMEM((rows, width), half)
    results = pl.pallas_call(
        functools.partial(kernel, devices, group, face_rows, chunk, block),
        out_shape=(
            pltpu.VMEM(faces.shape, jnp.float32),
            pltpu.VMEM(centres.shape, half),
            pltpu.VMEM(momentum.shape, half),
        ),
        in_specs=[hbm] * 4,
        out_specs=(vmem, vmem, vmem),
        scratch_shapes=[
            pltpu.VMEM((slot_rows, width), half),
            slots,
            pltpu.VMEM(labels.shape, jnp.int32),
            square, square, square,
            pltpu.VMEM((rows, 1), jnp.float32),
            pltpu.VMEM((rows, width), jnp.float32),
            slots, slots,
            pltpu.SemaphoreType.DMA((4,)),
            pltpu.SemaphoreType.DMA,
            pltpu.SemaphoreType.DMA,
            pltpu.SemaphoreType.DMA,
            pltpu.SemaphoreType.DMA,
        ],
        compiler_params=pltpu.CompilerParams(collective_id=0, has_side_effects=True),
    )(faces.transpose(1, 0, 2).reshape(slot_rows, width), labels, centres, momentum)
    anywhere = pl.BlockSpec(memory_space=pl.ANY)
    return pl.pallas_call(
        store_kernel,
        out_shape=tuple(jax.ShapeDtypeStruct(part.shape, part.dtype) for part in results),
        in_specs=[anywhere] * len(results),
        out_specs=(hbm,) * len(results),
        scratch_shapes=[pltpu.SemaphoreType.DMA((len(results),))],
    )(*(pltpu.with_memory_space_constraint(part, pltpu.VMEM) for part in results))


def solution(mesh):
    group = mesh.shape["cls"]
    devices = mesh.shape["dp"] * group
    in_specs = (P(None, ("dp", "cls"), None), P(), P(("dp", "cls"), None), P(("dp", "cls"), None))
    out_specs = (P(None, ("dp", "cls"), None), P(("dp", "cls"), None), P(("dp", "cls"), None))
    return jax.shard_map(
        functools.partial(local, devices, group),
        mesh=mesh, in_specs=in_specs, out_specs=out_specs, check_vma=False,
    )
```

```python
import functools
import jax
import jax.numpy as jnp
from jax import lax
from jax.experimental import pallas as pl
from jax.experimental.pallas import tpu as pltpu
from jax.sharding import PartitionSpec as P

SCALE = 30.0
MARGIN = 0.4
POS_WEIGHT = 0.7
BIAS = 6.5
EPS = 1e-06
MOMENTUM_RATE = 0.9
LEARN_RATE = 0.1
DECAY = 0.0005
MESH = pl.DeviceIdType.MESH


def logit_grad(cosine, positive):
    halfway = (cosine + 1.0) * 0.5
    square = halfway * halfway
    shaped = 2.0 * square * halfway - 1.0
    slopes = 3.0 * square
    argument = jnp.where(
        positive, -(SCALE * (shaped - MARGIN) + BIAS), SCALE * (shaped + MARGIN) + BIAS
    )
    weight = jnp.where(positive, -POS_WEIGHT * SCALE, (1.0 - POS_WEIGHT) * SCALE)
    return (weight * jax.nn.sigmoid(argument) * slopes).astype(jnp.bfloat16)


def kernel(
    devices, group, face_rows, chunk, block,
    faces_hbm, labels_hbm, centres_hbm, momentum_hbm,
    face_grad, new_centres, new_momentum,
    own, gathered, labels, centres, momentum, unit, inverse, grad, outgoing, incoming,
    local_sems, gather_send, gather_recv, scatter_send, scatter_recv,
):
    outer, inner = lax.axis_index("dp"), lax.axis_index("cls")
    me = outer * group + inner
    rows, width = centres.shape
    batches = labels.shape[0]
    slot_rows = batches * face_rows

    across = devices // group
    place = inner * across + outer

    def device(index):
        return (index // group, index % group)

    def early(step):
        spot = jnp.where(step >= place, step + 1, step)
        return (spot % across) * group + spot // across

    def late(step):
        return early(devices - 2 - step)

    load_faces = pltpu.make_async_copy(faces_hbm, own, local_sems.at[0])
    load_labels = pltpu.make_async_copy(labels_hbm, labels, local_sems.at[1])
    load_centres = pltpu.make_async_copy(centres_hbm, centres, local_sems.at[2])
    load_momentum = pltpu.make_async_copy(momentum_hbm, momentum, local_sems.at[3])
    load_faces.start()
    load_centres.start()
    load_labels.start()
    load_momentum.start()

    barrier = pltpu.get_barrier_semaphore()

    def greet(step, carry):
        peer = lax.rem(me + step, devices)
        pl.semaphore_signal(barrier, inc=1, device_id=device(peer), device_id_type=MESH)
        return carry

    lax.fori_loop(1, devices, greet, 0, unroll=devices <= 64)
    load_faces.wait()
    pl.semaphore_wait(barrier, devices - 1)

    def gather(step, carry):
        peer = late(step)
        pltpu.make_async_remote_copy(
            src_ref=own, dst_ref=gathered.at[me], send_sem=gather_send, recv_sem=gather_recv,
            device_id=device(peer), device_id_type=MESH,
        ).start()
        return carry

    lax.fori_loop(0, devices - 1, gather, 0, unroll=devices <= 64)
    pltpu.make_async_copy(own, gathered.at[me], gather_recv).start()

    load_centres.wait()

    def normalize(step, carry):
        part = pl.ds(pl.multiple_of(step * block, block), block)
        master = centres[part, :].astype(jnp.float32)
        scale = lax.rsqrt(jnp.sum(master * master, axis=1, keepdims=True) + EPS)
        inverse[part, :] = scale
        unit[part, :] = (master * scale).astype(jnp.bfloat16)
        return carry

    lax.fori_loop(0, rows // block, normalize, 0)
    load_labels.wait()
    count = chunk * slot_rows
    class_ids = me * rows + lax.broadcasted_iota(jnp.int32, (count, rows), 1)

    def label_column(first):
        shape = (count, labels.shape[1])
        row = lax.broadcasted_iota(jnp.int32, shape, 0)
        lane = lax.broadcasted_iota(jnp.int32, shape, 1)
        wanted = first * face_rows + row // batches
        batch = row % batches
        values = jnp.zeros(shape, jnp.float32)
        for number in range(batches):
            line = labels[number : number + 1, :].astype(jnp.float32)
            values = jnp.where((lane == wanted) & (batch == number), line, values)
        return jnp.sum(values, axis=1, keepdims=True).astype(jnp.int32)

    chunks = devices // chunk
    if chunks == 1:
        column = label_column(0)
    pltpu.make_async_copy(gathered, gathered, gather_recv).wait()

    def fold(step):
        if chunks == 1:
            slots = slice(None)
            target = column
        else:
            slots = pl.ds(step * chunk, chunk)
            target = label_column(step * chunk)
        piece = gathered[slots].reshape(count, width)
        cosine = lax.dot_general(
            piece, unit[...], (((1,), (1,)), ((), ())), preferred_element_type=jnp.float32
        )
        dlogit = logit_grad(cosine, target == class_ids)
        term = jnp.dot(dlogit, unit[...], preferred_element_type=jnp.float32)
        outgoing[slots] = term.astype(jnp.bfloat16).reshape(chunk, slot_rows, width)
        return dlogit, piece

    def outer_product(dlogit, piece):
        return lax.dot_general(
            dlogit, piece, (((0,), (0,)), ((), ())), preferred_element_type=jnp.float32
        )

    def scatter(step, carry):
        peer = early(step)
        pltpu.make_async_remote_copy(
            src_ref=outgoing.at[peer], dst_ref=incoming.at[me],
            send_sem=scatter_send, recv_sem=scatter_recv,
            device_id=device(peer), device_id_type=MESH,
        ).start()
        return carry

    if chunks == 1:
        dlogit, piece = fold(0)
        lax.fori_loop(0, devices - 1, scatter, 0, unroll=devices <= 64)
        pltpu.make_async_copy(outgoing.at[me], incoming.at[me], scatter_recv).start()
        grad[...] = outer_product(dlogit, piece)
    else:
        grad[...] = jnp.zeros_like(grad)

        def step_chunk(step, carry):
            dlogit, piece = fold(step)
            grad[...] += outer_product(dlogit, piece)
            return carry

        lax.fori_loop(0, chunks, step_chunk, 0)
        lax.fori_loop(0, devices - 1, scatter, 0)
        pltpu.make_async_copy(outgoing.at[me], incoming.at[me], scatter_recv).start()

    load_momentum.wait()

    def update(step, carry):
        part = pl.ds(pl.multiple_of(step * block, block), block)
        master = centres[part, :].astype(jnp.float32)
        scale = inverse[part, :]
        wide = master * scale
        grad_unit = grad[part, :]
        radial = jnp.sum(wide * grad_unit, axis=1, keepdims=True)
        grad_centre = (grad_unit - wide * radial) * scale
        velocity = (
            MOMENTUM_RATE * momentum[part, :].astype(jnp.float32) + grad_centre + DECAY * master
        )
        new_centres[part, :] = (master - LEARN_RATE * velocity).astype(jnp.bfloat16)
        new_momentum[part, :] = velocity.astype(jnp.bfloat16)
        return carry

    lax.fori_loop(0, rows // block, update, 0)
    pltpu.make_async_copy(incoming, incoming, scatter_recv).wait()
    if chunks == 1:
        total = jnp.sum(incoming[...].astype(jnp.float32), axis=0)
    else:
        total = lax.fori_loop(
            0, chunks,
            lambda step, sofar: sofar
            + jnp.sum(incoming[pl.ds(step * chunk, chunk)].astype(jnp.float32), axis=0),
            jnp.zeros((slot_rows, width), jnp.float32),
        )
    total = total.reshape(face_rows, batches, width)
    for batch in range(batches):
        face_grad[batch] = total[:, batch, :]

    if devices > 1:
        others = gathered.at[pl.ds(0, devices - 1)]
        pltpu.make_async_copy(others, others, gather_send).wait()
        others = outgoing.at[pl.ds(0, devices - 1)]
        pltpu.make_async_copy(others, others, scatter_send).wait()


def store_kernel(*refs):
    count = (len(refs) - 1) // 2
    sems = refs[-1]
    stores = [
        pltpu.make_async_copy(refs[number], refs[count + number], sems.at[number])
        for number in range(count)
    ]
    for store in stores:
        store.start()
    for store in stores:
        store.wait()


def local(devices, group, faces, labels, centres, momentum):
    batches, face_rows, width = faces.shape
    rows = centres.shape[0]
    slot_rows = batches * face_rows
    chunk = devices
    while chunk * slot_rows > 64 and chunk % 2 == 0:
        chunk //= 2
    block = 64 if rows % 64 == 0 else rows
    half = jnp.bfloat16
    hbm = pl.BlockSpec(memory_space=pltpu.HBM)
    vmem = pl.BlockSpec(memory_space=pltpu.VMEM)
    slots = pltpu.VMEM((devices, slot_rows, width), half)
    square = pltpu.VMEM((rows, width), half)
    results = pl.pallas_call(
        functools.partial(kernel, devices, group, face_rows, chunk, block),
        out_shape=(
            pltpu.VMEM(faces.shape, jnp.float32),
            pltpu.VMEM(centres.shape, half),
            pltpu.VMEM(momentum.shape, half),
        ),
        in_specs=[hbm] * 4,
        out_specs=(vmem, vmem, vmem),
        scratch_shapes=[
            pltpu.VMEM((slot_rows, width), half),
            slots,
            pltpu.VMEM(labels.shape, jnp.int32),
            square, square, square,
            pltpu.VMEM((rows, 1), jnp.float32),
            pltpu.VMEM((rows, width), jnp.float32),
            slots, slots,
            pltpu.SemaphoreType.DMA((4,)),
            pltpu.SemaphoreType.DMA,
            pltpu.SemaphoreType.DMA,
            pltpu.SemaphoreType.DMA,
            pltpu.SemaphoreType.DMA,
        ],
        compiler_params=pltpu.CompilerParams(collective_id=0, has_side_effects=True),
    )(faces.transpose(1, 0, 2).reshape(slot_rows, width), labels, centres, momentum)
    anywhere = pl.BlockSpec(memory_space=pl.ANY)
    return pl.pallas_call(
        store_kernel,
        out_shape=tuple(jax.ShapeDtypeStruct(part.shape, part.dtype) for part in results),
        in_specs=[anywhere] * len(results),
        out_specs=(hbm,) * len(results),
        scratch_shapes=[pltpu.SemaphoreType.DMA((len(results),))],
    )(*(pltpu.with_memory_space_constraint(part, pltpu.VMEM) for part in results))


def solution(mesh):
    group = mesh.shape["cls"]
    devices = mesh.shape["dp"] * group
    in_specs = (P(None, ("dp", "cls"), None), P(), P(("dp", "cls"), None), P(("dp", "cls"), None))
    out_specs = (P(None, ("dp", "cls"), None), P(("dp", "cls"), None), P(("dp", "cls"), None))
    return jax.shard_map(
        functools.partial(local, devices, group),
        mesh=mesh, in_specs=in_specs, out_specs=out_specs, check_vma=False,
    )
```
